32 devices in a mesh: ens: 4 (over y, x), space: 8 (over z, core).
Axes of the slice: x: 2, y: 2, z: 4, core: 2. Of those that a mesh axis runs over, the one named last changes fastest.
Arguments:
- latent: bfloat16 [16, 256, 8192], P('ens', None, 'space'), may hold values from -6 to 6
- noise: bfloat16 [16, 256, 8192], P('ens', None, 'space'), may hold values from -6 to 6
- target: float32 [224, 8192], P('ens', 'space'), may hold values from -6 to 6
- w_in: bfloat16 [384, 256], replicated, may hold values from -0.375 to 0.375
- w_out: bfloat16 [224, 384], replicated, may hold values from -0.3125 to 0.3125
- w_close_in: bfloat16 [384, 224], replicated, may hold values from -0.375 to 0.375
- w_close_out: bfloat16 [224, 384], replicated, may hold values from -0.3125 to 0.3125
Outputs:
- grad_latent: float32 [16, 256, 8192], P('ens', None, 'space')
- step_in: float32 [384, 256], replicated
- step_out: float32 [224, 384], replicated
- step_close_in: float32 [384, 224], replicated
- step_close_out: float32 [224, 384], replicated
The draws below stay inside these ranges and needn't reach their ends.
All inputs are finite; a program needn't handle non-finite values.
Results may differ from the reference program's by a relative error of at most 0.011.
Values sent between devices are 32-bit elements; how exact they have to be, the bound alone decides.
A program may use at most 128 MiB of HBM per device.

```python
import jax
import jax.numpy as jnp
from jax import lax

FIN = 256
HID = 384
MEMBERS = 16
K = 224
COLUMNS = 8192
NPAR = 356352


def levels(stream_key, dims, cuts, least, top_value):
    def one(axis_at, shards_of):
        draws = jax.random.uniform(jax.random.fold_in(jax.random.fold_in(stream_key, 6), axis_at), (shards_of,), jnp.float32, least / len(cuts), top_value / len(cuts))
        return jnp.repeat(jnp.exp(draws), dims[axis_at] // shards_of).reshape((-1,) + (1,) * (len(dims) - axis_at - 1))

    gain = one(*cuts[0])
    for cut in cuts[1:]:
        gain = gain * one(*cut)
    return gain


def scatter_about(key, shape, deviation, limit, shards=(), dtype=jnp.bfloat16):
    factor_of = levels(key, shape, shards, -0.22, 0.18) if shards else 1.0
    values = jax.random.normal(key, shape, jnp.float32) * deviation * factor_of
    return jnp.minimum(jnp.maximum(values, -limit), limit).astype(dtype)


def setup_inputs(seed: int = 0) -> dict:
    seeds = jax.random.split(jax.random.key(seed), 8)
    return {
        "latent": scatter_about(seeds[0], (MEMBERS, FIN, COLUMNS), 1.0, 6.0, ((0, 4), (2, 8))),
        "noise": scatter_about(seeds[1], (MEMBERS, FIN, COLUMNS), 1.0, 6.0, ((0, 4), (2, 8))),
        "target": scatter_about(seeds[2], (K, COLUMNS), 1.0, 6.0, ((0, 4), (1, 8)), jnp.float32),
        "w_in": scatter_about(seeds[3], (HID, FIN), FIN ** -0.5, 0.375),
        "w_out": scatter_about(seeds[4], (K, HID), HID ** -0.5, 0.3125),
        "w_close_in": scatter_about(seeds[5], (HID, K), K ** -0.5, 0.375),
        "w_close_out": scatter_about(seeds[6], (K, HID), HID ** -0.5, 0.3125),
    }


smooth_eps = 0.1

def activate(value):
    return jax.nn.gelu(value, approximate=True)

def activate_back(pre, grad):
    return jax.vjp(activate, pre)[1](grad)[0]

def smooth_sign(diff):
    return diff / jnp.sqrt(diff * diff + smooth_eps * smooth_eps)

def forward(zin, w_in, w_out, w_close_in, w_close_out):
    pre1 = jnp.dot(w_in, zin, preferred_element_type=jnp.float32)
    hid1 = activate(pre1).astype(jnp.bfloat16)
    dec = jnp.dot(w_out, hid1, preferred_element_type=jnp.float32)
    decb = dec.astype(jnp.bfloat16)
    pre3 = jnp.dot(w_close_in, decb, preferred_element_type=jnp.float32)
    hid3 = activate(pre3).astype(jnp.bfloat16)
    pred = dec + jnp.dot(w_close_out, hid3, preferred_element_type=jnp.float32)
    return (pre1, hid1, decb, pre3, hid3, pred)

def reference(latent, noise, target, w_in, w_out, w_close_in, w_close_out):
    zin_all = (latent.astype(jnp.float32) + 0.5 * noise.astype(jnp.float32)).astype(jnp.bfloat16)
    pred_all = lax.map(lambda zin: forward(zin, w_in, w_out, w_close_in, w_close_out)[5], zin_all)

    def pair_grad(mine):

        def add_one(index, total):
            other = lax.dynamic_index_in_dim(pred_all, index, 0, keepdims=False)
            return total + smooth_sign(mine - other)
        total = lax.fori_loop(0, MEMBERS, add_one, jnp.zeros_like(mine))
        return smooth_sign(mine - target) - total / MEMBERS
    gpred_all = lax.map(pair_grad, pred_all)

    def member_back(carry, inputs):
        zin, gpred = inputs
        pre1, hid1, decb, pre3, hid3, pred = forward(zin, w_in, w_out, w_close_in, w_close_out)
        gpredb = gpred.astype(jnp.bfloat16)
        g_close_out = jnp.dot(gpredb, hid3.T, preferred_element_type=jnp.float32)
        g_hid3 = jnp.dot(w_close_out.T, gpredb, preferred_element_type=jnp.float32)
        gpre3 = activate_back(pre3, g_hid3).astype(jnp.bfloat16)
        g_close_in = jnp.dot(gpre3, decb.T, preferred_element_type=jnp.float32)
        gdec = (gpred + jnp.dot(w_close_in.T, gpre3, preferred_element_type=jnp.float32)).astype(jnp.bfloat16)
        g_out = jnp.dot(gdec, hid1.T, preferred_element_type=jnp.float32)
        g_hid1 = jnp.dot(w_out.T, gdec, preferred_element_type=jnp.float32)
        gpre1 = activate_back(pre1, g_hid1).astype(jnp.bfloat16)
        g_in = jnp.dot(gpre1, zin.T, preferred_element_type=jnp.float32)
        g_latent = jnp.dot(w_in.T, gpre1, preferred_element_type=jnp.float32)
        carry = (carry[0] + g_in, carry[1] + g_out, carry[2] + g_close_in, carry[3] + g_close_out)
        return (carry, g_latent)
    start = (jnp.zeros((HID, FIN), jnp.float32), jnp.zeros((K, HID), jnp.float32), jnp.zeros((HID, K), jnp.float32), jnp.zeros((K, HID), jnp.float32))
    sums, grad_latent = lax.scan(member_back, start, (zin_all, gpred_all))
    squares = sum((jnp.sum(grad * grad) for grad in sums))
    rms = jnp.sqrt(squares / NPAR + 1e-12)
    return (grad_latent, sums[0] / rms, sums[1] / rms, sums[2] / rms, sums[3] / rms)
```

```python
import functools

import jax
import jax.numpy as jnp
from jax import lax
from jax.experimental import pallas as pl
from jax.experimental.pallas import tpu as pltpu
from jax.sharding import PartitionSpec as P

MESH = pl.DeviceIdType.MESH
EPS2 = 0.1 * 0.1
C0 = 0.7978845608028654
C1 = C0 * 0.044715
LANES = 128
F32 = jnp.float32
BF16 = jnp.bfloat16


def smooth_sign(diff):
    return diff * lax.rsqrt(diff * diff + EPS2)


def gelu_both(x):
    x2 = x * x
    t = jnp.tanh(x * (C0 + C1 * x2))
    half = 0.5 * x
    value = half + half * t
    slope = 0.5 + 0.5 * t + half * (1.0 - t * t) * (C0 + (3.0 * C1) * x2)
    return value, slope


def mm(a, b):
    return lax.dot_general(a, b, (((1,), (0,)), ((), ())), preferred_element_type=F32)


def mm_nt(a, b):
    return lax.dot_general(a, b, (((1,), (1,)), ((), ())), preferred_element_type=F32)


def step_kernel(
    ens,
    lat,
    noi,
    tgt,
    w_in,
    w_out,
    w_ci,
    w_co,
    w_in_t,
    w_out_t,
    w_ci_t,
    w_co_t,
    glat,
    gpack,
    zin_s,
    hid1_s,
    hid3_s,
    slope1_s,
    slope3_s,
    decb_s,
    out_pred,
    all_pred,
    out_grad,
    all_grad,
    t_in,
    t_all,
    gw_in,
    gw_out,
    gw_cit,
    gw_co,
    t_send,
    t_recv,
    p_send,
    p_recv,
    g_send,
    g_recv,
):
    members, fin, columns = lat.shape
    k = w_out.shape[0]
    rows_t = tgt.shape[0]
    share = columns // ens
    halves = share // LANES
    me = lax.axis_index("ens")
    sp = lax.axis_index("space")

    barrier = pltpu.get_barrier_semaphore()
    for t in range(1, ens):
        pl.semaphore_signal(
            barrier, inc=1, device_id=(lax.rem(me + t, ens), sp), device_id_type=MESH
        )
    pl.semaphore_wait(barrier, ens - 1)

    def target_copy(dst, src):
        return pltpu.make_async_remote_copy(
            src_ref=tgt.at[:, pl.ds(pl.multiple_of(dst * share, LANES), share)],
            dst_ref=t_in.at[src],
            send_sem=t_send.at[dst],
            recv_sem=t_recv.at[src],
            device_id=(dst, sp),
            device_id_type=MESH,
        )

    def pred_copy(h, dst, src):
        return pltpu.make_async_remote_copy(
            src_ref=out_pred.at[h, dst],
            dst_ref=all_pred.at[h, src],
            send_sem=p_send.at[h, dst],
            recv_sem=p_recv.at[h, src],
            device_id=(dst, sp),
            device_id_type=MESH,
        )

    def grad_copy(h, dst, src):
        return pltpu.make_async_remote_copy(
            src_ref=out_grad.at[h, dst],
            dst_ref=all_grad.at[h, src],
            send_sem=g_send.at[h, dst],
            recv_sem=g_recv.at[h, src],
            device_id=(dst, sp),
            device_id_type=MESH,
        )

    def forward(h, q):
        start = pl.multiple_of(q * share + h * LANES, LANES)
        cols = pl.ds(start, LANES)
        zin = jnp.concatenate(
            [
                (lat[m, :, cols].astype(F32) + 0.5 * noi[m, :, cols].astype(F32)).astype(BF16)
                for m in range(members)
            ],
            axis=1,
        )
        zin_s[h, q] = zin
        value, slope = gelu_both(mm(w_in[...], zin))
        hid1 = value.astype(BF16)
        hid1_s[h, q] = hid1
        slope1_s[h, q] = slope.astype(BF16)
        dec = mm(w_out[...], hid1)
        decb = dec.astype(BF16)
        decb_s[h, q] = decb
        value, slope = gelu_both(mm(w_ci[...], decb))
        hid3 = value.astype(BF16)
        hid3_s[h, q] = hid3
        slope3_s[h, q] = slope.astype(BF16)
        pred = dec + mm(w_co[...], hid3)
        for m in range(members):
            out_pred[h, q, m] = pred[:, m * LANES : (m + 1) * LANES]

    def pairs(h):
        count = ens * members

        def strip(r, carry):
            rows = pl.ds(pl.multiple_of(r * 8, 8), 8)
            x = [all_pred[h, i // members, i % members, rows, :] for i in range(count)]
            acc = [None] * count
            for i in range(count):
                for j in range(i + 1, count):
                    s = smooth_sign(x[i] - x[j])
                    acc[i] = s if acc[i] is None else acc[i] + s
                    acc[j] = -s if acc[j] is None else acc[j] - s
            truth = t_all[rows, h * LANES : (h + 1) * LANES]
            for i in range(count):
                out_grad[h, i // members, i % members, rows, :] = (
                    smooth_sign(x[i] - truth) - acc[i] * (1.0 / count)
                )
            return carry

        lax.fori_loop(0, k // 8, strip, 0)

    def backward(h, q):
        gp = jnp.concatenate([all_grad[h, q, m] for m in range(members)], axis=1)
        gpb = gp.astype(BF16)
        gw_co[...] += mm_nt(gpb, hid3_s[h, q])
        gpre3 = (slope3_s[h, q].astype(F32) * mm(w_co_t[...], gpb)).astype(BF16)
        gw_cit[...] += mm_nt(decb_s[h, q], gpre3)
        gdec = (gp + mm(w_ci_t[...], gpre3)).astype(BF16)
        gw_out[...] += mm_nt(gdec, hid1_s[h, q])
        gpre1 = (slope1_s[h, q].astype(F32) * mm(w_out_t[...], gdec)).astype(BF16)
        gw_in[...] += mm_nt(gpre1, zin_s[h, q])
        gl = mm(w_in_t[...], gpre1)
        cols = pl.ds(pl.multiple_of(q * share + h * LANES, LANES), LANES)
        for m in range(members):
            glat[m, :, cols] = gl[:, m * LANES : (m + 1) * LANES]

    for t in range(1, ens):
        target_copy(lax.rem(me + t, ens), me).start()
    t_in[me] = tgt[:, pl.ds(pl.multiple_of(me * share, LANES), share)]

    for h in range(halves):

        def go(t, carry, h=h):
            q = lax.rem(me + t, ens)
            forward(h, q)
            pred_copy(h, q, me).start()
            return carry

        lax.fori_loop(1, ens, go, 0)
        forward(h, me)
        all_pred[h, me] = out_pred[h, me]

    gw_in[...] = jnp.zeros_like(gw_in)
    gw_out[...] = jnp.zeros_like(gw_out)
    gw_cit[...] = jnp.zeros_like(gw_cit)
    gw_co[...] = jnp.zeros_like(gw_co)

    for t in range(1, ens):
        target_copy(lax.rem(me + t, ens), lax.rem(me + t, ens)).wait_recv()
    for e in range(ens):
        t_all[e * rows_t : (e + 1) * rows_t, :] = t_in[e]

    for h in range(halves):
        for t in range(1, ens):
            pred_copy(h, lax.rem(me + t, ens), lax.rem(me + t, ens)).wait_recv()
        pairs(h)
        for t in range(1, ens):
            grad_copy(h, lax.rem(me + t, ens), me).start()
        all_grad[h, me] = out_grad[h, me]

    for h in range(halves):

        def back(t, carry, h=h):
            q = lax.rem(me + t, ens)

            @pl.when(t > 0)
            def _():
                grad_copy(h, q, q).wait_recv()

            backward(h, q)
            return carry

        lax.fori_loop(0, ens, back, 0)

    for t in range(1, ens):
        target_copy(lax.rem(me + t, ens), me).wait_send()
        for h in range(halves):
            pred_copy(h, lax.rem(me + t, ens), me).wait_send()
            grad_copy(h, lax.rem(me + t, ens), me).wait_send()

    row = 0
    for ref in (gw_in, gw_out, gw_cit, gw_co):
        height, width = ref.shape
        for c in range(width // LANES):
            gpack[row : row + height, :] = ref[:, c * LANES : (c + 1) * LANES]
            row += height
    gpack[row:, :] = jnp.zeros((gpack.shape[0] - row, LANES), F32)


def reduce_kernel(
    ens,
    space,
    shapes,
    g,
    *refs,
):
    outs = refs[:4]
    part1, got1, part2, got2, got3, full, s1, r1, s2, r2, s3, r3, s4, r4, s5, r5, s6, r6 = refs[4:]
    rows = g.shape[0]
    half = rows // 2
    quarter = half // ens
    depth = space // 2
    piece = quarter // depth
    me = lax.axis_index("ens")
    sp = lax.axis_index("space")
    core = lax.rem(sp, 2)
    z = sp // 2
    mate = (me, sp + 1 - 2 * core)

    def at(start, size):
        return pl.ds(pl.multiple_of(start, 8), size)

    def ens_dev(e):
        return (e, sp)

    def z_dev(zz):
        return (me, zz * 2 + core)

    barrier = pltpu.get_barrier_semaphore()
    pl.semaphore_signal(barrier, inc=1, device_id=mate, device_id_type=MESH)
    for t in range(1, ens):
        pl.semaphore_signal(
            barrier, inc=1, device_id=ens_dev(lax.rem(me + t, ens)), device_id_type=MESH
        )
    for t in range(1, depth):
        pl.semaphore_signal(
            barrier, inc=1, device_id=z_dev(lax.rem(z + t, depth)), device_id_type=MESH
        )
    pl.semaphore_wait(barrier, 1 + (ens - 1) + (depth - 1))

    def copy(src, dst, send, recv, dev):
        return pltpu.make_async_remote_copy(
            src_ref=src, dst_ref=dst, send_sem=send, recv_sem=recv, device_id=dev, device_id_type=MESH
        )

    c1 = copy(g.at[at((1 - core) * half, half)], got1, s1.at[0], r1.at[0], mate)
    c1.start()
    c1.wait()
    part1[...] = g[at(core * half, half), :] + got1[...]

    def rs_ens(dst, src):
        return copy(part1.at[at(dst * quarter, quarter)], got2.at[src], s2.at[dst], r2.at[src], ens_dev(dst))

    for t in range(1, ens):
        rs_ens(lax.rem(me + t, ens), me).start()
    for t in range(1, ens):
        other = lax.rem(me + t, ens)
        rs_ens(other, other).wait_recv()
    total = part1[at(me * quarter, quarter), :]
    for t in range(1, ens):
        total = total + got2[lax.rem(me + t, ens)]
    part2[...] = total

    def rs_z(dst, src):
        return copy(part2.at[at(dst * piece, piece)], got3.at[src], s3.at[dst], r3.at[src], z_dev(dst))

    for t in range(1, depth):
        rs_z(lax.rem(z + t, depth), z).start()
    for t in range(1, depth):
        other = lax.rem(z + t, depth)
        rs_z(other, other).wait_recv()
    total = part2[at(z * piece, piece), :]
    for t in range(1, depth):
        total = total + got3[lax.rem(z + t, depth)]
    base = core * half + me * quarter
    full[at(base + z * piece, piece), :] = total

    def ag_z(dst, src):
        region = full.at[at(base + src * piece, piece)]
        return copy(region, region, s4.at[dst], r4.at[src], z_dev(dst))

    for t in range(1, depth):
        ag_z(lax.rem(z + t, depth), z).start()
    for t in range(1, depth):
        other = lax.rem(z + t, depth)
        ag_z(other, other).wait_recv()

    def ag_ens(dst, src):
        region = full.at[at(core * half + src * quarter, quarter)]
        return copy(region, region, s5.at[dst], r5.at[src], ens_dev(dst))

    for t in range(1, ens):
        ag_ens(lax.rem(me + t, ens), me).start()
    for t in range(1, ens):
        other = lax.rem(me + t, ens)
        ag_ens(other, other).wait_recv()

    mine = full.at[at(core * half, half)]
    c6 = copy(mine, mine, s6.at[0], r6.at[0], mate)
    c6.start()
    theirs = full.at[at((1 - core) * half, half)]
    copy(theirs, theirs, s6.at[0], r6.at[0], mate).wait_recv()

    c6.wait_send()
    for t in range(1, ens):
        other = lax.rem(me + t, ens)
        rs_ens(other, me).wait_send()
        ag_ens(other, me).wait_send()
    for t in range(1, depth):
        other = lax.rem(z + t, depth)
        rs_z(other, z).wait_send()
        ag_z(other, z).wait_send()

    used = sum(a * b for a, b in shapes) // LANES
    values = full[:used, :]
    squares = jnp.sum(values * values, keepdims=True)
    inverse = 1.0 / jnp.sqrt(squares / (used * LANES) + 1e-12)
    row = 0
    for out, (height, width) in zip(outs, shapes):
        for c in range(width // LANES):
            out[:, c * LANES : (c + 1) * LANES] = full[row : row + height, :] * inverse
            row += height


def body(ens, space, latent, noise, target, w_in, w_out, w_ci, w_co):
    members, fin, columns = latent.shape
    hid = w_in.shape[0]
    k = w_out.shape[0]
    rows_t = target.shape[0]
    share = columns // ens
    halves = share // LANES
    wide = members * LANES
    shapes = ((hid, fin), (k, hid), (k, hid), (k, hid))
    used = sum(a * b for a, b in shapes) // LANES
    unit = 8 * ens * space
    rows = -(-used // unit) * unit
    vmem = pl.BlockSpec(memory_space=pltpu.VMEM)
    dma = pltpu.SemaphoreType.DMA
    flops = 6 * 4 * hid * k * members * columns

    glat, gpack = pl.pallas_call(
        functools.partial(step_kernel, ens),
        name="crps_step",
        out_shape=(
            jax.ShapeDtypeStruct((members, fin, columns), F32),
            jax.ShapeDtypeStruct((rows, LANES), F32),
        ),
        in_specs=[vmem] * 11,
        out_specs=(vmem, vmem),
        scratch_shapes=[
            pltpu.VMEM((halves, ens, fin, wide), BF16),
            pltpu.VMEM((halves, ens, hid, wide), BF16),
            pltpu.VMEM((halves, ens, hid, wide), BF16),
            pltpu.VMEM((halves, ens, hid, wide), BF16),
            pltpu.VMEM((halves, ens, hid, wide), BF16),
            pltpu.VMEM((halves, ens, k, wide), BF16),
            pltpu.VMEM((halves, ens, members, k, LANES), F32),
            pltpu.VMEM((halves, ens, members, k, LANES), F32),
            pltpu.VMEM((halves, ens, members, k, LANES), F32),
            pltpu.VMEM((halves, ens, members, k, LANES), F32),
            pltpu.VMEM((ens, rows_t, share), F32),
            pltpu.VMEM((k, share), F32),
            pltpu.VMEM((hid, fin), F32),
            pltpu.VMEM((k, hid), F32),
            pltpu.VMEM((k, hid), F32),
            pltpu.VMEM((k, hid), F32),
            dma((ens,)),
            dma((ens,)),
            dma((halves, ens)),
            dma((halves, ens)),
            dma((halves, ens)),
            dma((halves, ens)),
        ],
        compiler_params=pltpu.CompilerParams(
            collective_id=0, has_side_effects=True, vmem_limit_bytes=58 * 2**20
        ),
        cost_estimate=pl.CostEstimate(flops=flops, bytes_accessed=2**24, transcendentals=2**24),
    )(latent, noise, target, w_in, w_out, w_ci, w_co, w_in.T, w_out.T, w_ci.T, w_co.T)

    half = rows // 2
    quarter = half // ens
    depth = space // 2
    piece = quarter // depth
    s_in, s_out, s_cit, s_co = pl.pallas_call(
        functools.partial(reduce_kernel, ens, space, shapes),
        name="weight_sum",
        out_shape=tuple(jax.ShapeDtypeStruct(s, F32) for s in shapes),
        in_specs=[vmem],
        out_specs=(vmem,) * 4,
        scratch_shapes=[
            pltpu.VMEM((half, LANES), F32),
            pltpu.VMEM((half, LANES), F32),
            pltpu.VMEM((quarter, LANES), F32),
            pltpu.VMEM((ens, quarter, LANES), F32),
            pltpu.VMEM((depth, piece, LANES), F32),
            pltpu.VMEM((rows, LANES), F32),
            dma((1,)),
            dma((1,)),
            dma((ens,)),
            dma((ens,)),
            dma((depth,)),
            dma((depth,)),
            dma((depth,)),
            dma((depth,)),
            dma((ens,)),
            dma((ens,)),
            dma((1,)),
            dma((1,)),
        ],
        compiler_params=pltpu.CompilerParams(
            collective_id=1, has_side_effects=True, vmem_limit_bytes=32 * 2**20
        ),
    )(gpack)
    return glat, s_in, s_out, s_cit.T, s_co


def solution(mesh):
    placed = (
        P("ens", None, "space"),
        P("ens", None, "space"),
        P("ens", "space"),
        P(),
        P(),
        P(),
        P(),
    )
    return jax.shard_map(
        functools.partial(body, mesh.shape["ens"], mesh.shape["space"]),
        mesh=mesh,
        in_specs=placed,
        out_specs=(P("ens", None, "space"), P(), P(), P(), P()),
        check_vma=False,
    )
```
